32 devices in a mesh: kpt: 4 (over x, core), row: 2 (over y), col: 4 (over z).
Axes of the slice: x: 2, y: 2, z: 4, core: 2. Of those that a mesh axis runs over, the one named last changes fastest.
Arguments:
- half_form: float32 [16, 2, 320, 2560], P('kpt', 'row', None, 'col'), parts along dimension 0, may hold values from -6 to 6
- panels: float32 [16, 2, 320, 2560], P('kpt', 'row'), parts along dimension 0, may hold values from -0.078125 to 0.078125
- inverse_blocks: float32 [16, 1, 2, 320, 640], P('kpt', None, 'row'), parts along dimension 0, may hold values from -0.25 to 0.25
Outputs:
- reduced: float32 [16, 2, 320, 2560], P('kpt', 'row', None, 'col'), parts along dimension 0
The draws below stay inside these ranges and needn't reach their ends.
There are 4 independent parts, one for each index of `kpt`. The reference program is written for one: setup_inputs(seed, part) draws one part's arguments, and reference() takes and returns one part's arrays. A program takes and returns all parts, laid end to end along the dimension named above; each array names one. Nothing has to cross between parts.
All inputs are finite; a program needn't handle non-finite values.
Results may differ from the reference program's by a relative error of at most 0.0001.
Values sent between devices are 32-bit elements; how exact they have to be, the bound alone decides.
No kernel may reach another device: no remote copies, remote signals or barrier semaphores. Data moves between devices by JAX's collectives and lax.ppermute only.
A program may use at most 64 MiB of HBM per device.

```python
import jax
import jax.numpy as jnp
from jax import lax

NB = 640
NT = 4
M = 2560
RB = 320
KB = 4
PR = 2
KT = 1


def steps_of(key, dims, pieces, smallest, largest):
    factor_of, own = 1.0, jax.random.fold_in(key, 6)
    for dim, blocks in pieces:
        heights = jnp.exp(jax.random.uniform(jax.random.fold_in(own, dim), (blocks,), jnp.float32, smallest / len(pieces), largest / len(pieces)))
        factor_of = factor_of * jnp.repeat(heights, dims[dim] // blocks).reshape([-1 if axis == dim else 1 for axis in range(len(dims))])
    return factor_of


def normal_values(stream_key, extent, width, limit, shards=(), kind=jnp.bfloat16):
    loudness = steps_of(stream_key, extent, shards, -0.22, 0.18) if shards else 1.0
    values = jax.random.normal(stream_key, extent, jnp.float32) * width * loudness
    return jnp.minimum(jnp.maximum(values, -limit), limit).astype(kind)


def setup_inputs(seed: int = 0, part: int = 0) -> dict:
    keys = jax.random.split(jax.random.key(seed), 4)
    own_keys = jax.random.split(jax.random.fold_in(keys[3], part), 4)
    return {
        "half_form": normal_values(own_keys[0], (KB, PR, RB, M), 1.0, 6.0, ((1, 2), (3, 4)), jnp.float32),
        "panels": normal_values(own_keys[1], (KB, PR, RB, M), (2 * M) ** -0.5, 0.078125, ((1, 2),), jnp.float32),
        "inverse_blocks": normal_values(own_keys[2], (NT, KT, PR, RB, NB), NB ** -0.5, 0.25, ((2, 2),), jnp.float32),
    }


def reference(half_form, panels, inverse_blocks):
    square = half_form.reshape(M, M)
    mirrored = square.T
    lower = panels.reshape(M, M)
    solved = []
    for tile in range(NT):
        remainder = mirrored[tile * NB:(tile + 1) * NB]
        if tile > 0:
            earlier = jnp.concatenate(solved, 0)
            remainder = remainder - jnp.dot(lower[tile * NB:(tile + 1) * NB, :tile * NB], earlier, precision=lax.Precision.HIGHEST, preferred_element_type=jnp.float32)
        inverse = inverse_blocks[tile].reshape(NB, NB).T
        solved.append(jnp.dot(inverse, remainder, precision=lax.Precision.HIGHEST, preferred_element_type=jnp.float32))
    return jnp.concatenate(solved, 0).reshape(half_form.shape)
```

```python
import jax
import jax.numpy as jnp
from jax import lax
from jax.sharding import PartitionSpec as P


def product(a, b, contract):
    return lax.dot_general(
        a,
        b,
        (contract, ((), ())),
        precision=lax.Precision.HIGH,
        preferred_element_type=jnp.float32,
    )


def partners(size, step):
    if size & (size - 1) == 0:
        return [(i, i ^ step) for i in range(size)]
    return [(i, (i + step) % size) for i in range(size)]


def columns_of_own_rows(half_form):
    blocks, _, stride, width = half_form.shape
    size = lax.axis_size("col")
    me = lax.axis_index("col")
    power = size & (size - 1) == 0
    received = []
    for step in reversed(range(size)):
        target = me ^ step if power else lax.rem(me + step, size)
        block = lax.dynamic_index_in_dim(half_form, target, 0, keepdims=False)[0]
        if step:
            block = lax.ppermute(block, "col", partners(size, step))
        received.insert(0, block)
    return received


def paired(half_form, panels, inverse_blocks):
    tiles, _, stride, width = half_form.shape
    order = panels.shape[-1]
    tile_order = inverse_blocks.shape[-1]
    row, col = lax.axis_index("row"), lax.axis_index("col")
    size = lax.axis_size("col")
    odd = col % 2
    piece = stride // 2
    received = columns_of_own_rows(half_form)
    swap_row = [(0, 1), (1, 0)]
    swap_col = [(i, i ^ 1) for i in range(size)]

    own_inverse = inverse_blocks[:, 0, 0]
    own_lower = panels[:, 0]
    inverse_parts, lower_parts = {}, {}

    def spread(block, alone):
        if alone:
            other = lax.ppermute(block, "row", swap_row)
            return (
                lax.dynamic_slice_in_dim(other, odd * piece, piece, 0),
                lax.dynamic_slice_in_dim(other, (1 - odd) * piece, piece, 0),
            )
        mine = lax.ppermute(
            lax.dynamic_slice_in_dim(block, odd * piece, piece, 0), "row", swap_row
        )
        return mine, lax.ppermute(mine, "col", swap_col)

    for tile in range(tiles):
        if tile:
            part = own_lower[tile, :, : tile * tile_order]
            lower_parts[tile] = (part, *spread(part, False))
        part = own_inverse[tile]
        inverse_parts[tile] = (part, *spread(part, tile == tiles - 1))

    mine_at = (1 - row) * stride + odd * piece
    near_at = (1 - row) * stride + (1 - odd) * piece
    solved, outputs = None, []
    for tile in range(tiles):
        which = col ^ tile
        columns = received[0]
        for step in range(1, size):
            columns = jnp.where(which == step, received[step], columns)
        columns = columns.T
        pieces = (
            lax.dynamic_slice_in_dim(columns, row * stride, stride, 0),
            lax.dynamic_slice_in_dim(columns, mine_at, piece, 0),
            lax.dynamic_slice_in_dim(columns, near_at, piece, 0),
        )
        total = 0.0
        for index, remainder in enumerate(pieces):
            if tile:
                remainder = remainder - product(lower_parts[tile][index], solved, ((1,), (0,)))
            total = total + product(inverse_parts[tile][index], remainder, ((0,), (0,)))
        solved = total if tile == 0 else jnp.concatenate([solved, total], 0)
        kept = lax.dynamic_slice_in_dim(total, row * stride, stride, 0)
        other = lax.ppermute(
            lax.dynamic_slice_in_dim(total, (1 - row) * stride, stride, 0), "row", swap_row
        )
        outputs.append(
            jnp.where(
                row == 0,
                jnp.concatenate([kept, other], 1),
                jnp.concatenate([other, kept], 1),
            )
        )
    return jnp.stack(outputs)[:, None]


def gathered(half_form, panels, inverse_blocks):
    blocks, _, stride, width = half_form.shape
    order = panels.shape[-1]
    tile_order = inverse_blocks.shape[-1]
    tiles = order // tile_order
    ranks = lax.axis_size("row")
    received = columns_of_own_rows(half_form)
    size, me = lax.axis_size("col"), lax.axis_index("col")
    power = size & (size - 1) == 0
    stacked = jnp.stack(received)
    own = jnp.arange(size)
    source = me ^ own if power else (me - own) % size
    mirrored = jnp.take(stacked, source, axis=0).transpose(0, 2, 1).reshape(order, stride)
    deep = blocks // tiles
    inverse = lax.all_gather(inverse_blocks, "row", axis=2, tiled=True).reshape(tiles, tile_order, tile_order)
    solved = None
    for tile in range(tiles):
        rows = slice(tile * tile_order, (tile + 1) * tile_order)
        remainder = mirrored[rows]
        if tile:
            own = panels[tile * deep : (tile + 1) * deep, :, :, : tile * tile_order]
            lower = lax.all_gather(own, "row", axis=1, tiled=True).reshape(tile_order, -1)
            remainder = remainder - product(lower, solved, ((1,), (0,)))
        total = product(inverse[tile], remainder, ((0,), (0,)))
        solved = total if tile == 0 else jnp.concatenate([solved, total], 0)
    pieces = solved.reshape(blocks, ranks, stride, stride)
    moved = lax.all_to_all(pieces, "row", split_axis=1, concat_axis=1, tiled=True)
    return moved.transpose(0, 2, 1, 3).reshape(blocks, 1, stride, width)


def on_device(half_form, panels, inverse_blocks):
    size = lax.axis_size("col")
    simple = (
        lax.axis_size("row") == 2
        and size % 2 == 0
        and size & (size - 1) == 0
        and half_form.shape[0] == size
        and inverse_blocks.shape[1] == 1
        and half_form.shape[2] % 2 == 0
    )
    return (paired if simple else gathered)(half_form, panels, inverse_blocks)


def solution(mesh):
    placed = (
        P("kpt", "row", None, "col"),
        P("kpt", "row", None, None),
        P("kpt", None, "row", None, None),
    )
    return jax.shard_map(
        on_device,
        mesh=mesh,
        in_specs=placed,
        out_specs=P("kpt", "row", None, "col"),
        check_vma=False,
    )
```
